512 devices in a mesh: dp: 8 (over y, core), tensor: 64 (over z, x).
Axes of the slice: x: 4, y: 4, z: 16, core: 2. Of those that a mesh axis runs over, the one named last changes fastest.
Arguments:
- hidden_states: bfloat16 [8192, 2560], P(('dp', 'tensor')), may hold values from -8 to 8
- norm_gain: float32 [2560], replicated, may hold values from 0.5 to 1.5
- head_weight: bfloat16 [2560, 76032], P('dp', 'tensor'), may hold values from -8 to 8
- targets: int32 [8192], P(('dp', 'tensor')), may hold values from 0 to 76031
- lengths: int32 [8, 16], P('dp'), may hold values from 1 to 512, 1024 in all within a row
Outputs:
- log_prob: float32 [8192], P(('dp', 'tensor'))
- entropy: float32 [8192], P(('dp', 'tensor'))
- seq_mean: float32 [8, 16], P('dp')
The draws below stay inside these ranges and needn't reach their ends.
Inputs may be any that keep to these rules, and one draw needn't show every extreme that they name: Each data group's lengths sum to 16 * 64.
All inputs are finite; a program needn't handle non-finite values.
Results may differ from the reference program's by a relative error of at most 0.0072.
Values may be sent and summed in bfloat16 or wider, within the bound.
A program may use at most 64 MiB of HBM per device.

```python
import math
import jax
import jax.numpy as jnp
import numpy as np
from jax import lax

D = 2560
ROW_DEV = 16
SEQS = 16
VOCAB = 76032
ROWS = 8192
N_DP = 8
N_TENSOR = 64


def sign_table(key):
    bits = jax.random.randint(jax.random.fold_in(key, 11), (D, VOCAB), 0, 2)
    return (bits * 2 - 1).astype(jnp.float32)


def head_matrix(key):
    base = jax.random.normal(jax.random.fold_in(key, 7), (D, VOCAB), jnp.float32) * (5.0 / math.sqrt(D))
    base = jnp.clip(base, -8.0, 8.0)
    columns = jnp.arange(VOCAB, dtype=jnp.int32)
    hot = columns % 97 == 3
    tier = 1.0 + 0.3 * (columns // 97 % 3).astype(jnp.float32)
    amplitude = jnp.minimum(280.0 * tier / D, 8.0)
    return jnp.where(hot[None, :], sign_table(key) * amplitude[None, :], base)


def draw_head_weight(key, part):
    return head_matrix(key).astype(jnp.bfloat16)


def draw_hidden_states(key, part):
    base_rows = jnp.clip(jax.random.normal(jax.random.fold_in(key, 3), (ROWS, D), jnp.float32), -6.0, 6.0)
    signs = sign_table(key)
    hot_count = (VOCAB - 4) // 97 + 1
    row_index = jnp.arange(ROWS, dtype=jnp.int32)
    first_col = 3 + 97 * (row_index * 7 % (hot_count - 3))
    second_col = first_col + 291
    aligned = jnp.transpose(signs[:, first_col] + 0.99 * signs[:, second_col]) + 0.03 * base_rows
    chosen = row_index % 61 == 5
    rows_out = jnp.where(chosen[:, None], aligned, base_rows)
    return jnp.clip(rows_out, -8.0, 8.0).astype(jnp.bfloat16)


def place_ends(entries, key, low, largest):
    longest = entries.shape.index(max(entries.shape))
    spots = []
    for shift in (0, 1):
        where = [jax.random.randint(jax.random.fold_in(key, axis), (), 0, length) for axis, length in enumerate(entries.shape)]
        where[longest] = (where[longest] + shift) % entries.shape[longest]
        spots.append(tuple(where))
    return entries.at[spots[0]].set(low).at[spots[1]].set(largest)


def ranked_wide(stream_key, shape, count, lean):
    loads = [min(1 << octave, count + 1 - (1 << octave)) * (1 << 20) // math.isqrt((1 << octave) ** lean) + 1 for octave in range((count + 1).bit_length()) if 1 << octave <= count]
    deviation = 1 + sum(loads) // (1 << 30)
    table = np.cumsum(np.array([max(1, weight // deviation) for weight in loads]))
    ticket = jax.random.randint(jax.random.fold_in(stream_key, 1), shape, 0, int(table[len(loads) - 1]))
    start = jnp.left_shift(1, jnp.searchsorted(jnp.asarray(table, jnp.int32), ticket, side="right").astype(jnp.int32))
    rank = start - 1 + jax.random.randint(jax.random.fold_in(stream_key, 4), shape, 0, 1 << 30) % jnp.minimum(start, count + 1 - start)
    return jax.random.permutation(jax.random.fold_in(stream_key, 2), count)[rank].astype(jnp.int32)


def split_up(count, total, reach, lean):
    weights = [(1 << 20) // math.isqrt(grade ** lean) + 1 for grade in range(2, count + 1)]
    rest, given = total - reach - (count - 1), [1] * (count - 1)
    while rest > 0:
        movable = [i for i in range(count - 1) if given[i] < reach]
        whole, left = sum([weights[i] for i in movable]), rest
        for i in movable:
            extra = min(reach - given[i], max(1, left * weights[i] // whole), rest)
            given[i] = given[i] + extra
            rest = rest - extra
    return np.array([reach] + given)


def uneven(key, amount, total, most, skew):
    if amount == 2:
        one = jax.random.randint(key, (), max(1, total - most), min(most, total - 1) + 1)
        return jnp.stack([one, total - one])
    sizes = jnp.asarray(split_up(amount, total, most, skew), jnp.int32)
    twos = (amount - 1) // 2
    giver, sink = sizes[1:1 + 2 * twos:2], sizes[2:2 + 2 * twos:2]
    margin = jnp.minimum(giver - 1, most - sink)
    shifted = jax.random.randint(jax.random.fold_in(key, 1), (twos,), 0, 1 << 20) % (margin + 1)
    sizes = sizes.at[1:1 + 2 * twos:2].set(giver - shifted).at[2:2 + 2 * twos:2].set(sink + shifted)
    return sizes[jax.random.permutation(jax.random.fold_in(key, 2), amount)]


def setup_inputs(seed: int = 0) -> dict:
    keys = jax.random.split(jax.random.key(seed), 6)
    hidden_states = draw_hidden_states(jax.random.fold_in(keys[5], 71), 0)
    norm_gain = jnp.clip(1.0 + 0.1 * jax.random.normal(keys[1], (D,), jnp.float32), 0.5, 1.5)
    head_weight = draw_head_weight(jax.random.fold_in(keys[5], 71), 0)
    targets = place_ends(ranked_wide(keys[3], (ROWS,), VOCAB, 2), jax.random.fold_in(keys[3], 3), 0, VOCAB - 1).astype(jnp.int32)
    lengths = jax.vmap(lambda own: uneven(own, SEQS, ROW_DEV * N_TENSOR, ROW_DEV * N_TENSOR // 2, 4))(jax.random.split(keys[4], N_DP)).reshape((N_DP, SEQS)).astype(jnp.int32)
    return {"hidden_states": hidden_states, "norm_gain": norm_gain, "head_weight": head_weight, "targets": targets, "lengths": lengths}


def sequence_sums(values, first_row, seq_lengths, seq_count):
    positions = first_row + jnp.arange(values.shape[0], dtype=jnp.int32)
    seq_ends = jnp.cumsum(seq_lengths).astype(jnp.int32)
    segment = lax.optimization_barrier(jnp.sum((positions[:, None] >= seq_ends[None, :]).astype(jnp.int32), axis=1))
    onehot = segment[:, None] == jnp.arange(seq_count, dtype=jnp.int32)[None, :]
    return lax.optimization_barrier(jnp.sum(jnp.where(onehot, values[:, None], 0.0), axis=0))

def reference(hidden_states, norm_gain, head_weight, targets, lengths):
    widths = hidden_states.astype(jnp.float32)
    meansq = lax.optimization_barrier(jnp.mean(widths * widths, axis=1, keepdims=True))
    normed = (widths * lax.rsqrt(meansq + 1e-06) * norm_gain).astype(jnp.bfloat16)

    def score_block(couple):
        block_rows, wanted = couple
        logits = jnp.dot(block_rows, head_weight, preferred_element_type=jnp.float32)
        highest = lax.optimization_barrier(jnp.max(logits, axis=1, keepdims=True))
        lse = highest + jnp.log(lax.optimization_barrier(jnp.sum(jnp.exp(logits - highest), axis=1, keepdims=True)))
        probability = jnp.exp(logits - lse)
        entropy_rows = lse[:, 0] - lax.optimization_barrier(jnp.sum(probability * logits, axis=1))
        picked = jnp.take_along_axis(logits, wanted[:, None].astype(jnp.int32), axis=1)[:, 0]
        return (picked - lse[:, 0], entropy_rows)
    log_prob, entropy = lax.map(score_block, (normed.reshape(-1, ROW_DEV, D), targets.reshape(-1, ROW_DEV)))
    log_prob = log_prob.reshape(-1)
    entropy = entropy.reshape(-1)

    def group_sums(group_values, group_lengths):
        return sequence_sums(group_values, 0, group_lengths, SEQS)
    sums = jax.vmap(group_sums)(log_prob.reshape(N_DP, -1), lengths)
    seq_mean = sums / lengths.astype(jnp.float32)
    return (log_prob, entropy, seq_mean)
```

```python
import functools

import jax
import jax.numpy as jnp
from jax import lax
from jax.experimental import pallas as pl
from jax.experimental.pallas import tpu as pltpu
from jax.sharding import PartitionSpec as P

MESH = pl.DeviceIdType.MESH
NX = 4
NY = 4
LANES = 128
CHUNKS = 4
EVENTS = 6


def split_columns(width):
    tiles = width // LANES
    first = max(1, round(tiles * 0.4)) * LANES
    rest = (width - first) // LANES + 1
    return first, first + rest // 2 * LANES


def kernel(nz, hidden_ref, gain_ref, w_hbm, targets_ref, lens_ref, lensv_ref,
           logp_ref, ent_ref, mean_ref,
           rows, wts, logits, stats, ex, sz_own, sz_a, sx_a, sx1, sx2, sw, sc, sex, ssend, sload):
    own_rows, width = hidden_ref.shape
    vocab = w_hbm.shape[-1]
    half = nz // 2
    ca, cm = split_columns(width)
    wide = width + LANES

    t = lax.axis_index("tensor")
    d = lax.axis_index("dp")
    z, x = t // NX, t % NX
    y, c = d // 2, d % 2
    zg = nz // 4

    def tensor_at(zz, xx):
        return {"tensor": zz * NX + xx}

    def dp_at(yy, cc):
        return {"dp": yy * 2 + cc}

    right, left = lax.rem(x + 1, NX), lax.rem(x + NX - 1, NX)
    across = lax.rem(x + 2, NX)
    up, down = lax.rem(z + 1, nz), lax.rem(z + nz - 1, nz)
    north, south = lax.rem(y + 1, NY), lax.rem(y + NY - 1, NY)

    load = pltpu.make_async_copy(w_hbm, wts.at[d], sload)
    load.start()

    barrier = pltpu.get_barrier_semaphore()
    peers = [tensor_at(z, right), tensor_at(z, left), tensor_at(z, across),
             tensor_at(up, x), tensor_at(down, x),
             dp_at(north, c), dp_at(south, c), dp_at(y, 1 - c)]
    peers += [tensor_at(z // 4 * 4 + lax.rem(z + i, 4), x) for i in (1, 2, 3)]
    peers += [tensor_at(lax.rem(z // 4 + i, zg) * 4 + z % 4, x) for i in range(1, zg)]
    for peer in peers:
        pl.semaphore_signal(barrier, inc=1, device_id=peer, device_id_type=MESH)

    widths = hidden_ref[...].astype(jnp.float32)
    meansq = jnp.sum(widths * widths, axis=1, keepdims=True) / width
    normed = widths * lax.rsqrt(meansq + 1e-06) * gain_ref[...]
    rows[z, x, :, 0:width] = normed.astype(jnp.bfloat16)
    row_id = lax.broadcasted_iota(jnp.int32, (own_rows, LANES), 0)
    lane = lax.broadcasted_iota(jnp.int32, (own_rows, LANES), 1)
    ids = jnp.zeros((own_rows, LANES), jnp.int32)
    for i in range(own_rows):
        ids = jnp.where(row_id == i, targets_ref[i], ids)
    digits = jnp.where(lane == 0, ids >> 16, jnp.where(lane == 1, (ids >> 8) & 255, ids & 255))
    digits = jnp.where(lane < 3, digits, 0)
    rows[z, x, :, width:wide] = digits.astype(jnp.float32).astype(jnp.bfloat16)

    pl.semaphore_wait(barrier, len(peers))

    def push(ref, send, recv, peer):
        pltpu.make_async_remote_copy(
            src_ref=ref, dst_ref=ref, send_sem=send, recv_sem=recv,
            device_id=peer, device_id_type=MESH,
        ).start()

    def got(ref, sem):
        pltpu.make_async_copy(ref, ref, sem).wait()

    def send_own(zo, to, way, step):
        push(rows.at[zo, x], ssend.at[0], sz_own.at[way, step], tensor_at(to, x))

    def send_a(zo, to, way, step):
        for i in (1, 2, 3):
            xo = lax.rem(x + i, NX)
            push(rows.at[zo, xo, :, pl.ds(0, ca)], ssend.at[1], sz_a.at[way, step], tensor_at(to, x))

    three_a = rows.at[0, pl.ds(0, 3), :, pl.ds(0, ca)]

    def send_x(zo):
        block = rows.at[zo, x, :, pl.ds(ca, wide - ca)]
        push(block, ssend.at[3], sx1.at[0, zo], tensor_at(z, right))
        push(block, ssend.at[3], sx1.at[1, zo], tensor_at(z, left))

    def forward_x(zo):
        got(rows.at[zo, left, :, pl.ds(ca, wide - ca)], sx1.at[0, zo])
        push(rows.at[zo, left, :, pl.ds(ca, cm - ca)], ssend.at[4], sx2.at[0, zo], tensor_at(z, right))
        got(rows.at[zo, right, :, pl.ds(ca, wide - ca)], sx1.at[1, zo])
        push(rows.at[zo, right, :, pl.ds(cm, wide - cm)], ssend.at[5], sx2.at[1, zo], tensor_at(z, left))

    def weight_event(j):
        for way in (0, 1):
            hop = 1 + j // CHUNKS
            yo = lax.rem(y + (NY - hop if way == 0 else hop), NY)
            piece = lax.rem(j + 2 * way, CHUNKS)
            ref = wts.at[yo * 2 + c, piece]
            got(ref, sw.at[way, j])

            @pl.when(j < 2)
            def _():
                push(ref, ssend.at[6], sw.at[way, j + CHUNKS], dp_at(north if way == 0 else south, c))

            push(ref, ssend.at[7], sc.at[way, j], dp_at(y, 1 - c))

    send_own(z, up, 0, 1)
    send_own(z, down, 1, 1)
    for i, (xo, slot) in enumerate(((right, 0), (left, 1), (across, 2))):
        push(rows.at[z, x, :, pl.ds(0, ca)], ssend.at[2], sx_a.at[slot], tensor_at(z, xo))
    send_x(z)
    load.wait()
    for j in range(CHUNKS):
        push(wts.at[d, j], ssend.at[6], sw.at[0, j], dp_at(north, c))
        piece = (j + 2) % CHUNKS
        push(wts.at[d, piece], ssend.at[6], sw.at[1, j], dp_at(south, c))
    for j in range(CHUNKS):
        push(wts.at[d, j], ssend.at[7], sc.at[2, j], dp_at(y, 1 - c))
    got(rows.at[z, left, :, pl.ds(0, ca)], sx_a.at[0])
    got(rows.at[z, right, :, pl.ds(0, ca)], sx_a.at[1])
    got(rows.at[z, across, :, pl.ds(0, ca)], sx_a.at[2])
    send_a(z, up, 0, 1)
    send_a(z, down, 1, 1)

    def ring_step(k, _):
        below, above = lax.rem(z + nz - k, nz), lax.rem(z + k, nz)
        got(rows.at[below, x], sz_own.at[0, k])
        send_own(below, up, 0, k + 1)
        got(rows.at[above, x], sz_own.at[1, k])

        @pl.when(k < half - 1)
        def _():
            send_own(above, down, 1, k + 1)

        send_x(below)
        send_x(above)
        got(three_a, sz_a.at[0, k])

        @pl.when(k < half - 1)
        def _():
            send_a(below, up, 0, k + 1)

        got(three_a, sz_a.at[1, k])
        send_a(above, down, 1, k + 1)

        forward_x(lax.rem(z + nz - k + 1, nz))

        @pl.when(k > 1)
        def _():
            forward_x(lax.rem(z + k - 1, nz))

        @pl.when(k <= EVENTS)
        def _():
            weight_event(k - 1)

        return 0

    lax.fori_loop(1, half, ring_step, 0)
    far = lax.rem(z + half, nz)
    got(rows.at[far, x], sz_own.at[0, half])
    send_x(far)
    if half > 1:
        forward_x(lax.rem(z + half + 1, nz))
    if half > 2:
        forward_x(lax.rem(z + half - 1, nz))
    for j in range(half - 1, EVENTS):
        weight_event(jnp.int32(j))
    got(three_a, sz_a.at[1, half])
    forward_x(far)

    def last_x(zo, _):
        got(rows.at[zo, across, :, pl.ds(ca, cm - ca)], sx2.at[0, zo])
        got(rows.at[zo, across, :, pl.ds(cm, wide - cm)], sx2.at[1, zo])
        return 0

    lax.fori_loop(0, nz, last_x, 0)

    def last_w(j, _):
        got(wts.at[0, 0], sc.at[0, j])
        got(wts.at[0, 0], sc.at[1, j])
        return 0

    lax.fori_loop(0, EVENTS, last_w, 0)
    for j in range(CHUNKS):
        got(wts.at[0, 0], sc.at[2, j])

    zs = 256 // (NX * own_rows)
    block = 256
    vocab_start = t * vocab
    lane_w = lax.broadcasted_iota(jnp.int32, (1, LANES), 1)
    digit_weights = jnp.where(lane_w == 0, 65536.0, jnp.where(lane_w == 1, 256.0, jnp.where(lane_w == 2, 1.0, 0.0)))

    def score(b, _):
        held = rows.at[pl.ds(b * zs, zs)]
        lhs = held[:, :, :, 0:width].reshape(block, width)
        rhs = wts[...].reshape(width, vocab)
        logits[...] = jnp.dot(lhs, rhs, preferred_element_type=jnp.float32)
        coded = held[:, :, :, width:wide].reshape(block, LANES).astype(jnp.float32)
        wanted = jnp.sum(coded * digit_weights, axis=1, keepdims=True).astype(jnp.int32) - vocab_start
        values = logits[...]
        highest = jnp.max(values, axis=1, keepdims=True)
        expo = jnp.exp(values - highest)
        total = jnp.sum(expo, axis=1, keepdims=True)
        weighted = jnp.sum(expo * values, axis=1, keepdims=True)
        columns = lax.broadcasted_iota(jnp.int32, values.shape, 1)
        picked = jnp.sum(jnp.where(columns == wanted, values, 0.0), axis=1, keepdims=True)
        at = lax.broadcasted_iota(jnp.int32, (block, LANES), 1)
        table = jnp.where(at == 0, highest, jnp.where(at == 1, total, jnp.where(at == 2, weighted, picked)))
        flat = jnp.transpose(table)
        for s in range(4):
            for q in range(block // LANES):
                stats[s, pl.ds(b * (block // LANES) + q, 1), :] = flat[s:s + 1, q * LANES:(q + 1) * LANES]
        return 0

    lax.fori_loop(0, nz // zs, score, 0)

    def exchange(stage, mine, size, peer_of):
        ex[stage, mine] = stats[...]
        for i in range(1, size):
            push(ex.at[stage, mine], ssend.at[8], sex.at[stage], peer_of(lax.rem(mine + i, size)))
        if size > 1:
            got(ex.at[stage, pl.ds(0, size - 1)], sex.at[stage])
        top = ex[stage, 0, 0]
        for i in range(1, size):
            top = jnp.maximum(top, ex[stage, i, 0])
        sums = [jnp.zeros_like(top) for _ in range(3)]
        for i in range(size):
            factor = jnp.exp(ex[stage, i, 0] - top)
            sums[0] += ex[stage, i, 1] * factor
            sums[1] += ex[stage, i, 2] * factor
            sums[2] += ex[stage, i, 3]
        stats[0] = top
        for i in range(3):
            stats[i + 1] = sums[i]

    exchange(0, x, NX, lambda i: tensor_at(z, i))
    exchange(1, z % 4, 4, lambda i: tensor_at(z // 4 * 4 + i, x))
    exchange(2, z // 4, zg, lambda i: tensor_at(i * 4 + z % 4, x))

    lse = stats[0] + jnp.log(stats[1])
    group_logp = stats[3] - lse
    group_ent = lse - stats[2] / stats[1]
    shape = group_logp.shape
    stats[0] = group_logp
    stats[1] = group_ent
    per = LANES // own_rows
    turn = lax.rem(LANES - t % per * own_rows, LANES)
    for ref, s in ((logp_ref, 0), (ent_ref, 1)):
        line = stats[s, pl.ds(t // per, 1), :]
        ref[...] = pltpu.roll(jnp.broadcast_to(line, (8, LANES)), turn, 1)[0:1, 0:own_rows]

    position = lax.broadcasted_iota(jnp.int32, shape, 0) * LANES + lax.broadcasted_iota(jnp.int32, shape, 1)
    count = lens_ref.shape[1]
    slot = lax.broadcasted_iota(jnp.int32, (1, count), 1)
    sums = jnp.zeros((1, count), jnp.float32)
    start = jnp.int32(0)
    for q in range(count):
        end = start + lens_ref[0, q]
        inside = (position >= start) & (position < end)
        part = jnp.sum(jnp.sum(jnp.where(inside, group_logp, 0.0), axis=0, keepdims=True), axis=1, keepdims=True)
        sums = jnp.where(slot == q, part, sums)
        start = end
    mean_ref[...] = sums / lensv_ref[...].astype(jnp.float32)

    got(rows.at[pl.ds(0, nz - 1), 0], ssend.at[0])
    got(rows.at[pl.ds(0, nz - 1), pl.ds(0, 3), :, pl.ds(0, ca)], ssend.at[1])
    got(three_a, ssend.at[2])
    got(rows.at[:, pl.ds(0, 2), :, pl.ds(ca, wide - ca)], ssend.at[3])
    got(rows.at[:, 0, :, pl.ds(ca, cm - ca)], ssend.at[4])
    got(rows.at[:, 0, :, pl.ds(cm, wide - cm)], ssend.at[5])
    got(wts.at[pl.ds(0, 3)], ssend.at[6])
    got(wts.at[pl.ds(0, 4)], ssend.at[7])
    for stage, size in ((0, NX), (1, 4), (2, zg)):
        if size > 1:
            got(ex.at[stage, pl.ds(0, size - 1)], ssend.at[8])


def on_device(nz, hidden_states, norm_gain, head_weight, targets, lengths):
    own_rows, width = hidden_states.shape
    depth, vocab = head_weight.shape
    wide = width + LANES
    group_rows = nz * NX * own_rows
    vmem = pl.BlockSpec(memory_space=pltpu.VMEM)
    smem = pl.BlockSpec(memory_space=pltpu.SMEM)
    dma = pltpu.SemaphoreType.DMA
    logp, ent, mean = pl.pallas_call(
        functools.partial(kernel, nz),
        out_shape=(
            jax.ShapeDtypeStruct((1, own_rows), jnp.float32),
            jax.ShapeDtypeStruct((1, own_rows), jnp.float32),
            jax.ShapeDtypeStruct(lengths.shape, jnp.float32),
        ),
        in_specs=[vmem, vmem, pl.BlockSpec(memory_space=pl.ANY), smem, smem, vmem],
        out_specs=(vmem, vmem, vmem),
        scratch_shapes=[
            pltpu.VMEM((nz, NX, own_rows, wide), jnp.bfloat16),
            pltpu.VMEM((2 * NY, CHUNKS, depth // CHUNKS, vocab), jnp.bfloat16),
            pltpu.VMEM((256, vocab), jnp.float32),
            pltpu.VMEM((4, group_rows // LANES, LANES), jnp.float32),
            pltpu.VMEM((3, 4, 4, group_rows // LANES, LANES), jnp.float32),
            dma((2, nz // 2 + 1)),
            dma((2, nz // 2 + 1)),
            dma((3,)),
            dma((2, nz)),
            dma((2, nz)),
            dma((2, EVENTS)),
            dma((3, EVENTS)),
            dma((3,)),
            dma((9,)),
            dma,
        ],
        compiler_params=pltpu.CompilerParams(
            collective_id=0, has_side_effects=True, vmem_limit_bytes=48 << 20
        ),
    )(hidden_states, norm_gain[None, :], head_weight.reshape(CHUNKS, depth // CHUNKS, vocab),
      targets, lengths, lengths)
    return logp[0], ent[0], mean


def solution(mesh):
    in_specs = (
        P(("dp", "tensor"), None),
        P(),
        P("dp", "tensor"),
        P(("dp", "tensor")),
        P("dp", None),
    )
    out_specs = (P(("dp", "tensor")), P(("dp", "tensor")), P("dp", None))
    return jax.shard_map(
        functools.partial(on_device, mesh.shape["tensor"] // NX),
        mesh=mesh, in_specs=in_specs, out_specs=out_specs, check_vma=False,
    )
```

```python
import functools

import jax
import jax.numpy as jnp
from jax import lax
from jax.experimental import pallas as pl
from jax.experimental.pallas import tpu as pltpu
from jax.sharding import PartitionSpec as P

MESH = pl.DeviceIdType.MESH
NX = 4
NY = 4
LANES = 128
CHUNKS = 4
EVENTS = 6


def split_columns(width):
    tiles = width // LANES
    first = max(1, round(tiles * 0.4)) * LANES
    rest = (width - first) // LANES + 1
    return first, first + rest // 2 * LANES


def kernel(nz, hidden_hbm, gain_hbm, w_hbm, targets_hbm, lens_hbm,
           out_ref,
           hidden_ref, gain_ref, targets_ref, lens_ref,
           rows, wts, logits, stats, ex, sz_b, sz_a, sx_a, sx1, sx2, sw, sc, sex, ssend, sload):
    own_rows, width = hidden_ref.shape
    vocab = w_hbm.shape[-1]
    half = nz // 2
    ca, cm = split_columns(width)
    wide = width + LANES

    t = lax.axis_index("tensor")
    d = lax.axis_index("dp")
    z, x = t // NX, t % NX
    y, c = d // 2, d % 2
    zg = nz // 4

    def tensor_at(zz, xx):
        return {"tensor": zz * NX + xx}

    def dp_at(yy, cc):
        return {"dp": yy * 2 + cc}

    right, left = lax.rem(x + 1, NX), lax.rem(x + NX - 1, NX)
    across = lax.rem(x + 2, NX)
    up, down = lax.rem(z + 1, nz), lax.rem(z + nz - 1, nz)
    north, south = lax.rem(y + 1, NY), lax.rem(y + NY - 1, NY)

    loads = [
        pltpu.make_async_copy(src, dst, sload.at[i])
        for i, (src, dst) in enumerate((
            (hidden_hbm, hidden_ref), (gain_hbm, gain_ref), (targets_hbm, targets_ref),
            (lens_hbm, lens_ref), (w_hbm, wts.at[d])))
    ]
    for load in loads:
        load.start()

    barrier = pltpu.get_barrier_semaphore()
    peers = [tensor_at(z, right), tensor_at(z, left), tensor_at(z, across),
             tensor_at(up, x), tensor_at(down, x),
             dp_at(north, c), dp_at(south, c), dp_at(y, 1 - c)]
    for peer in peers:
        pl.semaphore_signal(barrier, inc=1, device_id=peer, device_id_type=MESH)

    for load in loads[:4]:
        load.wait()
    widths = hidden_ref[...].astype(jnp.float32)
    meansq = jnp.sum(widths * widths, axis=1, keepdims=True) / width
    scaled = widths * lax.rsqrt(meansq + 1e-06)
    for i in range(width // LANES):
        cols = slice(i * LANES, (i + 1) * LANES)
        rows[z, x, :, cols] = (scaled[:, cols] * gain_ref[i:i + 1, :]).astype(jnp.bfloat16)
    row_id = lax.broadcasted_iota(jnp.int32, (own_rows, LANES), 0)
    lane = lax.broadcasted_iota(jnp.int32, (own_rows, LANES), 1)
    ids = jnp.zeros((own_rows, LANES), jnp.int32)
    for i in range(own_rows):
        ids = jnp.where(row_id == i, targets_ref[i], ids)
    digits = jnp.where(lane == 0, ids >> 16, jnp.where(lane == 1, (ids >> 8) & 255, ids & 255))
    digits = jnp.where(lane < 3, digits, 0)
    rows[z, x, :, width:wide] = digits.astype(jnp.float32).astype(jnp.bfloat16)

    pl.semaphore_wait(barrier, len(peers))

    def push(ref, send, recv, peer):
        pltpu.make_async_remote_copy(
            src_ref=ref, dst_ref=ref, send_sem=send, recv_sem=recv,
            device_id=peer, device_id_type=MESH,
        ).start()

    def got(ref, sem):
        pltpu.make_async_copy(ref, ref, sem).wait()

    b_cols = (pl.ds(ca, cm - ca), pl.ds(cm, wide - cm))

    def b_piece(zo, i):
        return rows.at[zo, x, :, b_cols[i]]

    def a_piece(zo, i):
        return rows.at[zo, lax.rem(x + (0, 1, 3, 2)[i], NX), :, pl.ds(0, ca)]

    def send_b(zo, to, way, step, i):
        push(b_piece(zo, i), ssend.at[i], sz_b.at[way, i, step], tensor_at(to, x))

    def send_a(zo, to, way, step, i):
        push(a_piece(zo, i), ssend.at[9], sz_a.at[way, i, step], tensor_at(to, x))

    def send_x(zo):
        block = rows.at[zo, x, :, pl.ds(ca, wide - ca)]
        push(block, ssend.at[3], sx1.at[0, zo], tensor_at(z, right))
        push(block, ssend.at[3], sx1.at[1, zo], tensor_at(z, left))

    def forward_x(zo):
        got(rows.at[zo, left, :, pl.ds(ca, wide - ca)], sx1.at[0, zo])
        push(rows.at[zo, left, :, pl.ds(ca, cm - ca)], ssend.at[4], sx2.at[0, zo], tensor_at(z, right))
        got(rows.at[zo, right, :, pl.ds(ca, wide - ca)], sx1.at[1, zo])
        push(rows.at[zo, right, :, pl.ds(cm, wide - cm)], ssend.at[5], sx2.at[1, zo], tensor_at(z, left))

    def weight_event(j):
        for way in (0, 1):
            hop = 1 + j // CHUNKS
            yo = lax.rem(y + (NY - hop if way == 0 else hop), NY)
            piece = lax.rem(j + 2 * way, CHUNKS)
            ref = wts.at[yo * 2 + c, piece]
            got(ref, sw.at[way, j])

            @pl.when(j < 2)
            def _():
                push(ref, ssend.at[6], sw.at[way, j + CHUNKS], dp_at(north if way == 0 else south, c))

            push(ref, ssend.at[7], sc.at[way, j], dp_at(y, 1 - c))

    for i in range(2):
        send_b(z, up, 0, 1, i)
        send_b(z, down, 1, 1, i)
    for i, (xo, slot) in enumerate(((right, 0), (left, 1), (across, 2))):
        push(rows.at[z, x, :, pl.ds(0, ca)], ssend.at[2], sx_a.at[slot], tensor_at(z, xo))
    send_x(z)
    send_a(z, up, 0, 1, 0)
    send_a(z, down, 1, 1, 0)
    loads[4].wait()
    for j in range(CHUNKS):
        push(wts.at[d, j], ssend.at[6], sw.at[0, j], dp_at(north, c))
        piece = (j + 2) % CHUNKS
        push(wts.at[d, piece], ssend.at[6], sw.at[1, j], dp_at(south, c))
    for j in range(CHUNKS):
        push(wts.at[d, j], ssend.at[7], sc.at[2, j], dp_at(y, 1 - c))
    for i, (xo, slot) in enumerate(((right, 1), (left, 0), (across, 2))):
        got(rows.at[z, xo, :, pl.ds(0, ca)], sx_a.at[slot])
        send_a(z, up, 0, 1, i + 1)
        send_a(z, down, 1, 1, i + 1)

    def ring_step(k, _):
        below, above = lax.rem(z + nz - k, nz), lax.rem(z + k, nz)
        for i in range(2):
            got(b_piece(below, i), sz_b.at[0, i, k])

            @pl.when((k < half - 1) | (i == 0))
            def _():
                send_b(below, up, 0, k + 1, i)

            got(b_piece(above, i), sz_b.at[1, i, k])

            @pl.when((k < half - 1) | (i == 1))
            def _():
                send_b(above, down, 1, k + 1, i)

        send_x(below)
        send_x(above)
        for i in range(4):
            got(a_piece(below, i), sz_a.at[0, i, k])

            @pl.when((k < half - 1) | (i < 2))
            def _():
                send_a(below, up, 0, k + 1, i)

            got(a_piece(above, i), sz_a.at[1, i, k])

            @pl.when((k < half - 1) | (i >= 2))
            def _():
                send_a(above, down, 1, k + 1, i)

        forward_x(lax.rem(z + nz - k + 1, nz))

        @pl.when(k > 1)
        def _():
            forward_x(lax.rem(z + k - 1, nz))

        @pl.when((k > 1) & (k <= EVENTS + 1))
        def _():
            weight_event(k - 2)

        return 0

    lax.fori_loop(1, half, ring_step, 0)
    far = lax.rem(z + half, nz)
    got(b_piece(far, 0), sz_b.at[0, 0, half])
    got(b_piece(far, 1), sz_b.at[1, 1, half])
    send_x(far)
    if half > 1:
        forward_x(lax.rem(z + half + 1, nz))
    if half > 2:
        forward_x(lax.rem(z + half - 1, nz))
    for j in range(max(half - 2, 0), EVENTS):
        weight_event(jnp.int32(j))
    for i in range(4):
        got(a_piece(far, i), sz_a.at[i // 2, i, half])
    forward_x(far)

    def last_x(zo, _):
        got(rows.at[zo, across, :, pl.ds(ca, cm - ca)], sx2.at[0, zo])
        got(rows.at[zo, across, :, pl.ds(cm, wide - cm)], sx2.at[1, zo])
        return 0

    lax.fori_loop(0, nz, last_x, 0)

    def last_w(j, _):
        got(wts.at[0, 0], sc.at[0, j])
        got(wts.at[0, 0], sc.at[1, j])
        return 0

    lax.fori_loop(0, EVENTS, last_w, 0)
    for j in range(CHUNKS):
        got(wts.at[0, 0], sc.at[2, j])

    zs = 256 // (NX * own_rows)
    block = 256
    vocab_start = t * vocab
    lane_w = lax.broadcasted_iota(jnp.int32, (1, LANES), 1)
    digit_weights = jnp.where(lane_w == 0, 65536.0, jnp.where(lane_w == 1, 256.0, jnp.where(lane_w == 2, 1.0, 0.0)))

    def score(b, _):
        held = rows.at[pl.ds(b * zs, zs)]
        lhs = held[:, :, :, 0:width].reshape(block, width)
        rhs = wts[...].reshape(width, vocab)
        logits[...] = jnp.dot(lhs, rhs, preferred_element_type=jnp.float32)
        coded = held[:, :, :, width:wide].reshape(block, LANES).astype(jnp.float32)
        wanted = jnp.sum(coded * digit_weights, axis=1, keepdims=True).astype(jnp.int32) - vocab_start
        values = logits[...]
        highest = jnp.max(values, axis=1, keepdims=True)
        expo = jnp.exp(values - highest)
        total = jnp.sum(expo, axis=1, keepdims=True)
        weighted = jnp.sum(expo * values, axis=1, keepdims=True)
        columns = lax.broadcasted_iota(jnp.int32, values.shape, 1)
        picked = jnp.sum(jnp.where(columns == wanted, values, 0.0), axis=1, keepdims=True)
        at = lax.broadcasted_iota(jnp.int32, (block, LANES), 1)
        table = jnp.where(at == 0, highest, jnp.where(at == 1, total, jnp.where(at == 2, weighted, picked)))
        flat = jnp.transpose(table)
        for s in range(4):
            for q in range(block // LANES):
                stats[s, pl.ds(b * (block // LANES) + q, 1), :] = flat[s:s + 1, q * LANES:(q + 1) * LANES]
        return 0

    lax.fori_loop(0, nz // zs, score, 0)

    def exchange(stage, mine, size, peer_of):
        ex[stage, mine] = stats[...]
        for i in range(1, size):
            push(ex.at[stage, mine], ssend.at[8], sex.at[stage], peer_of(lax.rem(mine + i, size)))
        if size > 1:
            got(ex.at[stage, pl.ds(0, size - 1)], sex.at[stage])
        top = ex[stage, 0, 0]
        for i in range(1, size):
            top = jnp.maximum(top, ex[stage, i, 0])
        sums = [jnp.zeros_like(top) for _ in range(3)]
        for i in range(size):
            factor = jnp.exp(ex[stage, i, 0] - top)
            sums[0] += ex[stage, i, 1] * factor
            sums[1] += ex[stage, i, 2] * factor
            sums[2] += ex[stage, i, 3]
        stats[0] = top
        for i in range(3):
            stats[i + 1] = sums[i]

    exchange(0, x, NX, lambda i: tensor_at(z, i))
    exchange(1, z % 4, 4, lambda i: tensor_at(z // 4 * 4 + i, x))
    exchange(2, z // 4, zg, lambda i: tensor_at(i * 4 + z % 4, x))

    lse = stats[0] + jnp.log(stats[1])
    group_logp = stats[3] - lse
    group_ent = lse - stats[2] / stats[1]
    shape = group_logp.shape
    stats[0] = group_logp
    stats[1] = group_ent
    per = LANES // own_rows
    turn = lax.rem(LANES - t % per * own_rows, LANES)
    for s in range(2):
        line = stats[s, pl.ds(t // per, 1), :]
        out_ref[s:s + 1, :] = pltpu.roll(jnp.broadcast_to(line, (8, LANES)), turn, 1)[0:1, :]

    position = lax.broadcasted_iota(jnp.int32, shape, 0) * LANES + lax.broadcasted_iota(jnp.int32, shape, 1)
    count = lens_ref.shape[1]
    slot = lax.broadcasted_iota(jnp.int32, (1, LANES), 1)
    sums = jnp.zeros((1, LANES), jnp.float32)
    spans = jnp.ones((1, LANES), jnp.int32)
    start = jnp.int32(0)
    for q in range(count):
        end = start + lens_ref[0, q]
        inside = (position >= start) & (position < end)
        part = jnp.sum(jnp.sum(jnp.where(inside, group_logp, 0.0), axis=0, keepdims=True), axis=1, keepdims=True)
        sums = jnp.where(slot == q, part, sums)
        spans = jnp.where(slot == q, lens_ref[0, q], spans)
        start = end
    out_ref[2:3, :] = sums / spans.astype(jnp.float32)
    out_ref[3:8, :] = jnp.zeros((5, LANES), jnp.float32)

    for i in range(2):
        got(rows.at[pl.ds(0, nz - 1), 0, :, b_cols[i]], ssend.at[i])
    got(rows.at[pl.ds(0, nz - 1), :, :, pl.ds(0, ca)], ssend.at[9])
    got(rows.at[0, pl.ds(0, 3), :, pl.ds(0, ca)], ssend.at[2])
    got(rows.at[:, pl.ds(0, 2), :, pl.ds(ca, wide - ca)], ssend.at[3])
    got(rows.at[:, 0, :, pl.ds(ca, cm - ca)], ssend.at[4])
    got(rows.at[:, 0, :, pl.ds(cm, wide - cm)], ssend.at[5])
    got(wts.at[pl.ds(0, 3)], ssend.at[6])
    got(wts.at[pl.ds(0, 4)], ssend.at[7])
    for stage, size in ((0, NX), (1, 4), (2, zg)):
        if size > 1:
            got(ex.at[stage, pl.ds(0, size - 1)], ssend.at[8])


def on_device(nz, hidden_states, norm_gain, head_weight, targets, lengths):
    own_rows, width = hidden_states.shape
    depth, vocab = head_weight.shape
    wide = width + LANES
    group_rows = nz * NX * own_rows
    vmem = pl.BlockSpec(memory_space=pltpu.VMEM)
    hbm = pl.BlockSpec(memory_space=pltpu.HBM)
    dma = pltpu.SemaphoreType.DMA
    out = pl.pallas_call(
        functools.partial(kernel, nz),
        out_shape=jax.ShapeDtypeStruct((8, LANES), jnp.float32),
        in_specs=[hbm] * 5,
        out_specs=vmem,
        scratch_shapes=[
            pltpu.VMEM((own_rows, width), jnp.bfloat16),
            pltpu.VMEM((width // LANES, LANES), jnp.float32),
            pltpu.SMEM((own_rows,), jnp.int32),
            pltpu.SMEM(lengths.shape, jnp.int32),
            pltpu.VMEM((nz, NX, own_rows, wide), jnp.bfloat16),
            pltpu.VMEM((2 * NY, CHUNKS, depth // CHUNKS, vocab), jnp.bfloat16),
            pltpu.VMEM((256, vocab), jnp.float32),
            pltpu.VMEM((4, group_rows // LANES, LANES), jnp.float32),
            pltpu.VMEM((3, 4, 4, group_rows // LANES, LANES), jnp.float32),
            dma((2, 2, nz // 2 + 1)),
            dma((2, 4, nz // 2 + 1)),
            dma((3,)),
            dma((2, nz)),
            dma((2, nz)),
            dma((2, EVENTS)),
            dma((3, EVENTS)),
            dma((3,)),
            dma((10,)),
            dma((5,)),
        ],
        compiler_params=pltpu.CompilerParams(
            collective_id=0, has_side_effects=True, vmem_limit_bytes=64 << 20
        ),
    )(hidden_states, norm_gain.reshape(width // LANES, LANES),
      head_weight.reshape(CHUNKS, depth // CHUNKS, vocab), targets, lengths)
    return out[0, :own_rows], out[1, :own_rows], out[2:3, :lengths.shape[1]]


def solution(mesh):
    in_specs = (
        P(("dp", "tensor"), None),
        P(),
        P("dp", "tensor"),
        P(("dp", "tensor")),
        P("dp", None),
    )
    out_specs = (P(("dp", "tensor")), P(("dp", "tensor")), P("dp", None))
    return jax.shard_map(
        functools.partial(on_device, mesh.shape["tensor"] // NX),
        mesh=mesh, in_specs=in_specs, out_specs=out_specs, check_vma=False,
    )
```

```python
import functools

import jax
import jax.numpy as jnp
from jax import lax
from jax.experimental import pallas as pl
from jax.experimental.pallas import tpu as pltpu
from jax.sharding import PartitionSpec as P

MESH = pl.DeviceIdType.MESH
NX = 4
NY = 4
LANES = 128
CHUNKS = 4
EVENTS = 6


def split_columns(width):
    tiles = width // LANES
    first = max(1, round(tiles * 0.4)) * LANES
    rest = (width - first) // LANES + 1
    return first, first + rest // 2 * LANES


def kernel(nz, hidden_hbm, gain_hbm, w_hbm, targets_hbm, lens_hbm,
           out_ref,
           hidden_ref, gain_ref, targets_ref, lens_ref,
           rows, wts, logits, stats, ex_x, ex_z, done, sz_b, sz_a, sx_a, sx1, sx2, sw, sc, sex, ssend, sload):
    own_rows, width = hidden_ref.shape
    vocab = w_hbm.shape[-1]
    half = nz // 2
    ca, cm = split_columns(width)
    wide = width + LANES

    t = lax.axis_index("tensor")
    d = lax.axis_index("dp")
    z, x = t // NX, t % NX
    y, c = d // 2, d % 2

    def tensor_at(zz, xx):
        return {"tensor": zz * NX + xx}

    def dp_at(yy, cc):
        return {"dp": yy * 2 + cc}

    right, left = lax.rem(x + 1, NX), lax.rem(x + NX - 1, NX)
    across = lax.rem(x + 2, NX)
    up, down = lax.rem(z + 1, nz), lax.rem(z + nz - 1, nz)
    north, south = lax.rem(y + 1, NY), lax.rem(y + NY - 1, NY)

    loads = [
        pltpu.make_async_copy(src, dst, sload.at[i])
        for i, (src, dst) in enumerate((
            (hidden_hbm, hidden_ref), (gain_hbm, gain_ref), (targets_hbm, targets_ref),
            (lens_hbm, lens_ref), (w_hbm, wts.at[d])))
    ]
    for load in loads:
        load.start()

    barrier = pltpu.get_barrier_semaphore()
    peers = [tensor_at(z, right), tensor_at(z, left), tensor_at(z, across),
             tensor_at(up, x), tensor_at(down, x),
             dp_at(north, c), dp_at(south, c), dp_at(y, 1 - c)]
    for peer in peers:
        pl.semaphore_signal(barrier, inc=1, device_id=peer, device_id_type=MESH)

    for load in loads[:4]:
        load.wait()
    widths = hidden_ref[...].astype(jnp.float32)
    meansq = jnp.sum(widths * widths, axis=1, keepdims=True) / width
    scaled = widths * lax.rsqrt(meansq + 1e-06)
    for i in range(width // LANES):
        cols = slice(i * LANES, (i + 1) * LANES)
        rows[z, x, :, cols] = (scaled[:, cols] * gain_ref[i:i + 1, :]).astype(jnp.bfloat16)
    row_id = lax.broadcasted_iota(jnp.int32, (own_rows, LANES), 0)
    lane = lax.broadcasted_iota(jnp.int32, (own_rows, LANES), 1)
    ids = jnp.zeros((own_rows, LANES), jnp.int32)
    for i in range(own_rows):
        ids = jnp.where(row_id == i, targets_ref[i], ids)
    digits = jnp.where(lane == 0, ids >> 16, jnp.where(lane == 1, (ids >> 8) & 255, ids & 255))
    digits = jnp.where(lane < 3, digits, 0)
    rows[z, x, :, width:wide] = digits.astype(jnp.float32).astype(jnp.bfloat16)

    pl.semaphore_wait(barrier, len(peers))

    def push(ref, send, recv, peer):
        pltpu.make_async_remote_copy(
            src_ref=ref, dst_ref=ref, send_sem=send, recv_sem=recv,
            device_id=peer, device_id_type=MESH,
        ).start()

    def got(ref, sem):
        pltpu.make_async_copy(ref, ref, sem).wait()

    b_cols = (pl.ds(ca, cm - ca), pl.ds(cm, wide - cm))

    def b_piece(zo, i):
        return rows.at[zo, x, :, b_cols[i]]

    def a_piece(zo, i):
        return rows.at[zo, lax.rem(x + (0, 1, 3, 2)[i], NX), :, pl.ds(0, ca)]

    def send_b(zo, to, way, step, i):
        push(b_piece(zo, i), ssend.at[i], sz_b.at[way, i, step], tensor_at(to, x))

    def send_a(zo, to, way, step, i):
        push(a_piece(zo, i), ssend.at[9], sz_a.at[way, i, step], tensor_at(to, x))

    def send_x(zo):
        block = rows.at[zo, x, :, pl.ds(ca, wide - ca)]
        push(block, ssend.at[8], sx1.at[0, zo], tensor_at(z, right))
        push(block, ssend.at[8], sx1.at[1, zo], tensor_at(z, left))

    def forward_x(zo):
        got(rows.at[zo, left, :, pl.ds(ca, wide - ca)], sx1.at[0, zo])
        push(rows.at[zo, left, :, pl.ds(ca, cm - ca)], ssend.at[10], sx2.at[0, zo], tensor_at(z, right))
        got(rows.at[zo, right, :, pl.ds(ca, wide - ca)], sx1.at[1, zo])
        push(rows.at[zo, right, :, pl.ds(cm, wide - cm)], ssend.at[11], sx2.at[1, zo], tensor_at(z, left))

    def weight_event(j):
        for way in (0, 1):
            hop = 1 + j // CHUNKS
            yo = lax.rem(y + (NY - hop if way == 0 else hop), NY)
            piece = lax.rem(j + 2 * way, CHUNKS)
            ref = wts.at[yo * 2 + c, piece]
            got(ref, sw.at[way, j])

            @pl.when(j < 2)
            def _():
                push(ref, ssend.at[6], sw.at[way, j + CHUNKS], dp_at(north if way == 0 else south, c))

            push(ref, ssend.at[7], sc.at[way, j], dp_at(y, 1 - c))

    for i in range(2):
        send_b(z, up, 0, 1, i)
        send_b(z, down, 1, 1, i)
    for i, (xo, slot) in enumerate(((right, 0), (left, 1), (across, 2))):
        push(rows.at[z, x, :, pl.ds(0, ca)], ssend.at[2], sx_a.at[slot], tensor_at(z, xo))
    send_x(z)
    send_a(z, up, 0, 1, 0)
    send_a(z, down, 1, 1, 0)
    loads[4].wait()
    for j in range(CHUNKS):
        push(wts.at[d, j], ssend.at[6], sw.at[0, j], dp_at(north, c))
        piece = (j + 2) % CHUNKS
        push(wts.at[d, piece], ssend.at[6], sw.at[1, j], dp_at(south, c))
    for j in range(CHUNKS):
        push(wts.at[d, j], ssend.at[7], sc.at[2, j], dp_at(y, 1 - c))
    for i, (xo, slot) in enumerate(((right, 1), (left, 0), (across, 2))):
        got(rows.at[z, xo, :, pl.ds(0, ca)], sx_a.at[slot])
        send_a(z, up, 0, 1, i + 1)
        send_a(z, down, 1, 1, i + 1)

    def ring_step(k, _):
        below, above = lax.rem(z + nz - k, nz), lax.rem(z + k, nz)
        for i in range(2):
            got(b_piece(below, i), sz_b.at[0, i, k])

            @pl.when((k < half - 1) | (i == 0))
            def _():
                send_b(below, up, 0, k + 1, i)

            got(b_piece(above, i), sz_b.at[1, i, k])

            @pl.when((k < half - 1) | (i == 1))
            def _():
                send_b(above, down, 1, k + 1, i)

        send_x(below)
        send_x(above)
        for i in range(4):
            got(a_piece(below, i), sz_a.at[0, i, k])

            @pl.when((k < half - 1) | (i < 2))
            def _():
                send_a(below, up, 0, k + 1, i)

            got(a_piece(above, i), sz_a.at[1, i, k])

            @pl.when((k < half - 1) | (i >= 2))
            def _():
                send_a(above, down, 1, k + 1, i)

        forward_x(lax.rem(z + nz - k + 1, nz))

        @pl.when(k > 1)
        def _():
            forward_x(lax.rem(z + k - 1, nz))

        @pl.when((k > 1) & (k <= EVENTS + 1))
        def _():
            weight_event(k - 2)

        return 0

    lax.fori_loop(1, half, ring_step, 0)
    far = lax.rem(z + half, nz)
    got(b_piece(far, 0), sz_b.at[0, 0, half])
    got(b_piece(far, 1), sz_b.at[1, 1, half])
    send_x(far)
    if half > 1:
        forward_x(lax.rem(z + half + 1, nz))
    if half > 2:
        forward_x(lax.rem(z + half - 1, nz))
    for j in range(max(half - 2, 0), EVENTS):
        weight_event(jnp.int32(j))

    def last_w(j, _):
        got(wts.at[0, 0], sc.at[0, j])
        got(wts.at[0, 0], sc.at[1, j])
        return 0

    lax.fori_loop(0, EVENTS, last_w, 0)
    for j in range(CHUNKS):
        got(wts.at[0, 0], sc.at[2, j])

    pairs = nz // 2
    pair_rows = 2 * NX * own_rows
    vocab_start = t * vocab
    lane_w = lax.broadcasted_iota(jnp.int32, (1, LANES), 1)
    digit_weights = jnp.where(lane_w == 0, 65536.0, jnp.where(lane_w == 1, 256.0, jnp.where(lane_w == 2, 1.0, 0.0)))

    def score(j, _):
        @pl.when(j == 1)
        def _():
            for i in range(4):
                got(a_piece(far, i), sz_a.at[i // 2, i, half])
            forward_x(far)

        both = (lax.rem(z // 2 + pairs - j, pairs), lax.rem(z // 2 + 1 + j, pairs))
        for pair in both:
            for i in range(2):
                zo = pair * 2 + i
                got(rows.at[zo, across, :, b_cols[0]], sx2.at[0, zo])
                got(rows.at[zo, across, :, b_cols[1]], sx2.at[1, zo])
        held = [rows[pl.ds(pair * 2, 2)].reshape(pair_rows, wide) for pair in both]
        held = jnp.concatenate(held, axis=0)
        rhs = wts[...].reshape(width, vocab)
        logits[...] = jnp.dot(held[:, 0:width], rhs, preferred_element_type=jnp.float32)
        coded = held[:, width:wide].astype(jnp.float32)
        wanted = jnp.sum(coded * digit_weights, axis=1, keepdims=True).astype(jnp.int32) - vocab_start
        values = logits[...]
        highest = jnp.max(values, axis=1, keepdims=True)
        expo = jnp.exp(values - highest)
        total = jnp.sum(expo, axis=1, keepdims=True)
        weighted = jnp.sum(expo * values, axis=1, keepdims=True)
        columns = lax.broadcasted_iota(jnp.int32, values.shape, 1)
        picked = jnp.sum(jnp.where(columns == wanted, values, 0.0), axis=1, keepdims=True)
        at = lax.broadcasted_iota(jnp.int32, (2 * pair_rows, LANES), 1)
        table = jnp.where(at == 0, highest, jnp.where(at == 1, total, jnp.where(at == 2, weighted, picked)))
        flat = jnp.transpose(table)
        for i, pair in enumerate(both):
            for s in range(4):
                stats[pair // 2, pl.ds(2 * s + pair % 2, 1), :] = flat[s:s + 1, i * LANES:(i + 1) * LANES]
        return 0

    lax.fori_loop(0, pairs // 2, score, 0)

    def combine(held):
        top = held[0][0:2]
        for one in held[1:]:
            top = jnp.maximum(top, one[0:2])
        sums = [jnp.zeros_like(top) for _ in range(3)]
        for one in held:
            factor = jnp.exp(one[0:2] - top)
            sums[0] += one[2:4] * factor
            sums[1] += one[4:6] * factor
            sums[2] += one[6:8]
        return top, sums

    quarters = pairs // 2
    ex_x[x] = stats[x]
    for i in (1, 2, 3):
        xo = lax.rem(x + i, NX)
        pltpu.make_async_remote_copy(
            src_ref=stats.at[xo], dst_ref=ex_x.at[x], send_sem=ssend.at[3], recv_sem=sex.at[0],
            device_id=tensor_at(z, xo), device_id_type=MESH,
        ).start()
    got(ex_x.at[pl.ds(0, NX - 1)], sex.at[0])
    top, sums = combine([ex_x[i] for i in range(NX)])
    ex_z[z] = jnp.concatenate([top] + sums, axis=0)
    for i in range(1, nz):
        push(ex_z.at[z], ssend.at[4], sex.at[1], tensor_at(lax.rem(z + i, nz), x))
    got(ex_z.at[pl.ds(0, nz - 1)], sex.at[1])
    top, sums = combine([ex_z[i] for i in range(nz)])
    lse = top + jnp.log(sums[0])
    done[x, 0:2, :] = sums[2] - lse
    done[x, 2:4, :] = lse - sums[1] / sums[0]
    for i in (1, 2, 3):
        push(done.at[x], ssend.at[5], sex.at[2], tensor_at(z, lax.rem(x + i, NX)))
    got(done.at[pl.ds(0, NX - 1)], sex.at[2])
    group_logp = jnp.concatenate([done[i, 0:2] for i in range(quarters)], axis=0)
    shape = group_logp.shape
    per = LANES // own_rows
    turn = lax.rem(LANES - t % per * own_rows, LANES)
    for s in range(2):
        line = done[t // per // 2, pl.ds(2 * s + t // per % 2, 1), :]
        out_ref[s:s + 1, :] = pltpu.roll(jnp.broadcast_to(line, (8, LANES)), turn, 1)[0:1, :]

    position = lax.broadcasted_iota(jnp.int32, shape, 0) * LANES + lax.broadcasted_iota(jnp.int32, shape, 1)
    count = lens_ref.shape[1]
    slot = lax.broadcasted_iota(jnp.int32, (1, LANES), 1)
    sums = jnp.zeros((1, LANES), jnp.float32)
    spans = jnp.ones((1, LANES), jnp.int32)
    start = jnp.int32(0)
    for q in range(count):
        end = start + lens_ref[0, q]
        inside = (position >= start) & (position < end)
        part = jnp.sum(jnp.sum(jnp.where(inside, group_logp, 0.0), axis=0, keepdims=True), axis=1, keepdims=True)
        sums = jnp.where(slot == q, part, sums)
        spans = jnp.where(slot == q, lens_ref[0, q], spans)
        start = end
    out_ref[2:3, :] = sums / spans.astype(jnp.float32)
    out_ref[3:8, :] = jnp.zeros((5, LANES), jnp.float32)

    for i in range(2):
        got(rows.at[pl.ds(0, nz - 1), 0, :, b_cols[i]], ssend.at[i])
    got(rows.at[pl.ds(0, nz - 1), :, :, pl.ds(0, ca)], ssend.at[9])
    got(rows.at[0, pl.ds(0, 3), :, pl.ds(0, ca)], ssend.at[2])
    got(rows.at[:, pl.ds(0, 2), :, pl.ds(ca, wide - ca)], ssend.at[8])
    got(rows.at[:, 0, :, b_cols[0]], ssend.at[10])
    got(rows.at[:, 0, :, b_cols[1]], ssend.at[11])
    got(wts.at[pl.ds(0, 3)], ssend.at[6])
    got(wts.at[pl.ds(0, 4)], ssend.at[7])
    got(ex_x.at[pl.ds(0, NX - 1)], ssend.at[3])
    got(ex_z.at[pl.ds(0, nz - 1)], ssend.at[4])
    got(done.at[pl.ds(0, NX - 1)], ssend.at[5])


def on_device(nz, hidden_states, norm_gain, head_weight, targets, lengths):
    own_rows, width = hidden_states.shape
    depth, vocab = head_weight.shape
    wide = width + LANES
    group_rows = nz * NX * own_rows
    vmem = pl.BlockSpec(memory_space=pltpu.VMEM)
    hbm = pl.BlockSpec(memory_space=pltpu.HBM)
    dma = pltpu.SemaphoreType.DMA
    out = pl.pallas_call(
        functools.partial(kernel, nz),
        out_shape=jax.ShapeDtypeStruct((8, LANES), jnp.float32),
        in_specs=[hbm] * 5,
        out_specs=vmem,
        scratch_shapes=[
            pltpu.VMEM((own_rows, width), jnp.bfloat16),
            pltpu.VMEM((width // LANES, LANES), jnp.float32),
            pltpu.SMEM((own_rows,), jnp.int32),
            pltpu.SMEM(lengths.shape, jnp.int32),
            pltpu.VMEM((nz, NX, own_rows, wide), jnp.bfloat16),
            pltpu.VMEM((2 * NY, CHUNKS, depth // CHUNKS, vocab), jnp.bfloat16),
            pltpu.VMEM((256, vocab), jnp.float32),
            pltpu.VMEM((group_rows // LANES // 2, 8, LANES), jnp.float32),
            pltpu.VMEM((NX, 8, LANES), jnp.float32),
            pltpu.VMEM((nz, 8, LANES), jnp.float32),
            pltpu.VMEM((NX, 4, LANES), jnp.float32),
            dma((2, 2, nz // 2 + 1)),
            dma((2, 4, nz // 2 + 1)),
            dma((3,)),
            dma((2, nz)),
            dma((2, nz)),
            dma((2, EVENTS)),
            dma((3, EVENTS)),
            dma((3,)),
            dma((12,)),
            dma((5,)),
        ],
        compiler_params=pltpu.CompilerParams(
            collective_id=0, has_side_effects=True, vmem_limit_bytes=64 << 20
        ),
    )(hidden_states, norm_gain.reshape(width // LANES, LANES),
      head_weight.reshape(CHUNKS, depth // CHUNKS, vocab), targets, lengths)
    return out[0, :own_rows], out[1, :own_rows], out[2:3, :lengths.shape[1]]


def solution(mesh):
    in_specs = (
        P(("dp", "tensor"), None),
        P(),
        P("dp", "tensor"),
        P(("dp", "tensor")),
        P("dp", None),
    )
    out_specs = (P(("dp", "tensor")), P(("dp", "tensor")), P("dp", None))
    return jax.shard_map(
        functools.partial(on_device, mesh.shape["tensor"] // NX),
        mesh=mesh, in_specs=in_specs, out_specs=out_specs, check_vma=False,
    )
```

```python
import functools

import jax
import jax.numpy as jnp
from jax import lax
from jax.experimental import pallas as pl
from jax.experimental.pallas import tpu as pltpu
from jax.sharding import PartitionSpec as P

MESH = pl.DeviceIdType.MESH
NX = 4
NY = 4
LANES = 128
CHUNKS = 4
EVENTS = 6


def split_columns(width):
    tiles = width // LANES
    first = max(1, round(tiles * 0.4)) * LANES
    rest = (width - first) // LANES + 1
    return first, first + rest // 2 * LANES


def kernel(nz, hidden_hbm, gain_hbm, w_hbm, targets_hbm, lens_hbm,
           out_ref,
           hidden_ref, gain_ref, targets_ref, lens_ref,
           rows, wts, logits, stats, ex_x, ex_z, done, sz_b, sz_a, sx_a, sx1, sx2, sw, sc, sex, ssend, sload):
    own_rows, width = hidden_ref.shape
    vocab = w_hbm.shape[-1]
    half = nz // 2
    ca, cm = split_columns(width)
    wide = width + LANES

    t = lax.axis_index("tensor")
    d = lax.axis_index("dp")
    z, x = t // NX, t % NX
    y, c = d // 2, d % 2

    def tensor_at(zz, xx):
        return {"tensor": zz * NX + xx}

    def dp_at(yy, cc):
        return {"dp": yy * 2 + cc}

    right, left = lax.rem(x + 1, NX), lax.rem(x + NX - 1, NX)
    across = lax.rem(x + 2, NX)
    up, down = lax.rem(z + 1, nz), lax.rem(z + nz - 1, nz)
    north, south = lax.rem(y + 1, NY), lax.rem(y + NY - 1, NY)

    loads = [
        pltpu.make_async_copy(src, dst, sload.at[i])
        for i, (src, dst) in enumerate((
            (hidden_hbm, hidden_ref), (gain_hbm, gain_ref), (targets_hbm, targets_ref),
            (lens_hbm, lens_ref), (w_hbm, wts.at[d])))
    ]
    for load in loads:
        load.start()

    barrier = pltpu.get_barrier_semaphore()
    peers = [tensor_at(z, right), tensor_at(z, left), tensor_at(z, across),
             tensor_at(up, x), tensor_at(down, x),
             dp_at(north, c), dp_at(south, c), dp_at(y, 1 - c)]
    for peer in peers:
        pl.semaphore_signal(barrier, inc=1, device_id=peer, device_id_type=MESH)

    for load in loads[:4]:
        load.wait()
    widths = hidden_ref[...].astype(jnp.float32)
    meansq = jnp.sum(widths * widths, axis=1, keepdims=True) / width
    scaled = widths * lax.rsqrt(meansq + 1e-06)
    for i in range(width // LANES):
        cols = slice(i * LANES, (i + 1) * LANES)
        rows[z, x, :, cols] = (scaled[:, cols] * gain_ref[i:i + 1, :]).astype(jnp.bfloat16)
    row_id = lax.broadcasted_iota(jnp.int32, (own_rows, LANES), 0)
    lane = lax.broadcasted_iota(jnp.int32, (own_rows, LANES), 1)
    ids = jnp.zeros((own_rows, LANES), jnp.int32)
    for i in range(own_rows):
        ids = jnp.where(row_id == i, targets_ref[i], ids)
    digits = jnp.where(lane == 0, ids >> 16, jnp.where(lane == 1, (ids >> 8) & 255, ids & 255))
    digits = jnp.where(lane < 3, digits, 0)
    rows[z, x, :, width:wide] = digits.astype(jnp.float32).astype(jnp.bfloat16)

    pl.semaphore_wait(barrier, len(peers))

    def push(ref, send, recv, peer):
        pltpu.make_async_remote_copy(
            src_ref=ref, dst_ref=ref, send_sem=send, recv_sem=recv,
            device_id=peer, device_id_type=MESH,
        ).start()

    def got(ref, sem):
        pltpu.make_async_copy(ref, ref, sem).wait()

    b_cols = (pl.ds(ca, cm - ca), pl.ds(cm, wide - cm))

    def b_piece(zo, i):
        return rows.at[zo, x, :, b_cols[i]]

    def a_piece(zo, i):
        return rows.at[zo, lax.rem(x + (0, 1, 3, 2)[i], NX), :, pl.ds(0, ca)]

    def send_b(zo, to, way, step, i):
        push(b_piece(zo, i), ssend.at[i], sz_b.at[way, i, step], tensor_at(to, x))

    def send_a(zo, to, way, step, i):
        push(a_piece(zo, i), ssend.at[9], sz_a.at[way, i, step], tensor_at(to, x))

    def send_x(zo):
        block = rows.at[zo, x, :, pl.ds(ca, wide - ca)]
        push(block, ssend.at[8], sx1.at[0, zo], tensor_at(z, right))
        push(block, ssend.at[8], sx1.at[1, zo], tensor_at(z, left))

    def send_across(zo):
        for i in range(2):
            push(b_piece(zo, i), ssend.at[10 + i], sx2.at[i, zo], tensor_at(z, across))

    def got_sides(zo):
        got(rows.at[zo, left, :, pl.ds(ca, wide - ca)], sx1.at[0, zo])
        got(rows.at[zo, right, :, pl.ds(ca, wide - ca)], sx1.at[1, zo])

    def forward_x(zo):
        got(rows.at[zo, left, :, pl.ds(ca, wide - ca)], sx1.at[0, zo])
        push(rows.at[zo, left, :, pl.ds(ca, cm - ca)], ssend.at[10], sx2.at[0, zo], tensor_at(z, right))
        got(rows.at[zo, right, :, pl.ds(ca, wide - ca)], sx1.at[1, zo])
        push(rows.at[zo, right, :, pl.ds(cm, wide - cm)], ssend.at[11], sx2.at[1, zo], tensor_at(z, left))

    def weight_event(j):
        for way in (0, 1):
            hop = 1 + j // CHUNKS
            yo = lax.rem(y + (NY - hop if way == 0 else hop), NY)
            piece = lax.rem(j + 2 * way, CHUNKS)
            ref = wts.at[yo * 2 + c, piece]
            got(ref, sw.at[way, j])

            @pl.when(j < 2)
            def _():
                push(ref, ssend.at[6], sw.at[way, j + CHUNKS], dp_at(north if way == 0 else south, c))

            push(ref, ssend.at[7], sc.at[way, j], dp_at(y, 1 - c))

    for i in range(2):
        send_b(z, up, 0, 1, i)
        send_b(z, down, 1, 1, i)
    loads[4].wait()
    for j in range(CHUNKS):
        push(wts.at[d, j], ssend.at[6], sw.at[0, j], dp_at(north, c))
        piece = (j + 2) % CHUNKS
        push(wts.at[d, piece], ssend.at[6], sw.at[1, j], dp_at(south, c))
    for i, (xo, slot) in enumerate(((right, 0), (left, 1), (across, 2))):
        push(rows.at[z, x, :, pl.ds(0, ca)], ssend.at[2], sx_a.at[slot], tensor_at(z, xo))
    send_x(z)
    send_a(z, up, 0, 1, 0)
    send_a(z, down, 1, 1, 0)
    for j in range(CHUNKS):
        push(wts.at[d, j], ssend.at[7], sc.at[2, j], dp_at(y, 1 - c))
    for i, (xo, slot) in enumerate(((right, 1), (left, 0), (across, 2))):
        got(rows.at[z, xo, :, pl.ds(0, ca)], sx_a.at[slot])
        send_a(z, up, 0, 1, i + 1)
        send_a(z, down, 1, 1, i + 1)

    def ring_step(k, _):
        below, above = lax.rem(z + nz - k, nz), lax.rem(z + k, nz)
        for i in range(2):
            got(b_piece(below, i), sz_b.at[0, i, k])

            @pl.when((k < half - 1) | (i == 0))
            def _():
                send_b(below, up, 0, k + 1, i)

            got(b_piece(above, i), sz_b.at[1, i, k])

            @pl.when((k < half - 1) | (i == 1))
            def _():
                send_b(above, down, 1, k + 1, i)

        send_x(below)
        send_x(above)

        @pl.when(k == half - 1)
        def _():
            send_across(below)
            send_across(above)

        for i in range(4):
            got(a_piece(below, i), sz_a.at[0, i, k])

            @pl.when((k < half - 1) | (i < 2))
            def _():
                send_a(below, up, 0, k + 1, i)

            got(a_piece(above, i), sz_a.at[1, i, k])

            @pl.when((k < half - 1) | (i >= 2))
            def _():
                send_a(above, down, 1, k + 1, i)

        forward_x(lax.rem(z + nz - k + 1, nz))

        @pl.when(k > 1)
        def _():
            forward_x(lax.rem(z + k - 1, nz))

        @pl.when(k <= EVENTS)
        def _():
            weight_event(k - 1)

        return 0

    lax.fori_loop(1, half, ring_step, 0)
    far = lax.rem(z + half, nz)
    got(b_piece(far, 0), sz_b.at[0, 0, half])
    got(b_piece(far, 1), sz_b.at[1, 1, half])
    send_x(far)
    send_across(far)
    for j in range(half - 1, EVENTS):
        weight_event(jnp.int32(j))

    def last_w(j, _):
        got(wts.at[0, 0], sc.at[0, j])
        got(wts.at[0, 0], sc.at[1, j])
        return 0

    lax.fori_loop(0, EVENTS, last_w, 0)
    for j in range(CHUNKS):
        got(wts.at[0, 0], sc.at[2, j])

    pairs = nz // 2
    pair_rows = 2 * NX * own_rows
    vocab_start = t * vocab
    lane_w = lax.broadcasted_iota(jnp.int32, (1, LANES), 1)
    digit_weights = jnp.where(lane_w == 0, 65536.0, jnp.where(lane_w == 1, 256.0, jnp.where(lane_w == 2, 1.0, 0.0)))

    def pairs_of(j):
        return lax.rem(z // 2 + pairs - j, pairs), lax.rem(z // 2 + 1 + j, pairs)

    def arrived(j):
        if j == pairs // 2 - 2:
            got_sides(lax.rem(z + nz - half + 1, nz))
            got_sides(lax.rem(z + half - 1, nz))
        if j == pairs // 2 - 1:
            for i in range(4):
                got(a_piece(far, i), sz_a.at[i // 2, i, half])
            got_sides(far)
        for pair in pairs_of(j):
            for i in range(2):
                zo = pair * 2 + i
                got(rows.at[zo, across, :, b_cols[0]], sx2.at[0, zo])
                got(rows.at[zo, across, :, b_cols[1]], sx2.at[1, zo])

    def multiply(j):
        held = [rows[pl.ds(pair * 2, 2)].reshape(pair_rows, wide) for pair in pairs_of(j)]
        held = jnp.concatenate(held, axis=0)
        rhs = wts[...].reshape(width, vocab)
        logits[...] = jnp.dot(held[:, 0:width], rhs, preferred_element_type=jnp.float32)

    def summarize(j):
        both = pairs_of(j)
        coded = jnp.concatenate(
            [rows[pl.ds(pair * 2, 2), :, :, width:wide].reshape(pair_rows, LANES) for pair in both], axis=0
        ).astype(jnp.float32)
        wanted = jnp.sum(coded * digit_weights, axis=1, keepdims=True).astype(jnp.int32) - vocab_start
        values = logits[...]
        highest = jnp.max(values, axis=1, keepdims=True)
        expo = jnp.exp(values - highest)
        total = jnp.sum(expo, axis=1, keepdims=True)
        weighted = jnp.sum(expo * values, axis=1, keepdims=True)
        columns = lax.broadcasted_iota(jnp.int32, values.shape, 1)
        picked = jnp.sum(jnp.where(columns == wanted, values, 0.0), axis=1, keepdims=True)
        at = lax.broadcasted_iota(jnp.int32, (2 * pair_rows, LANES), 1)
        table = jnp.where(at == 0, highest, jnp.where(at == 1, total, jnp.where(at == 2, weighted, picked)))
        flat = jnp.transpose(table)
        for i, pair in enumerate(both):
            for s in range(4):
                stats[pair // 2, pl.ds(2 * s + pair % 2, 1), :] = flat[s:s + 1, i * LANES:(i + 1) * LANES]

    def score(j, _):
        for jj in range(pairs // 2):
            @pl.when(j == jj)
            def _():
                arrived(jj)

        multiply(j)
        summarize(j)
        return 0

    lax.fori_loop(0, pairs // 2, score, 0)

    def combine(held):
        top = held[0][0:2]
        for one in held[1:]:
            top = jnp.maximum(top, one[0:2])
        sums = [jnp.zeros_like(top) for _ in range(3)]
        for one in held:
            factor = jnp.exp(one[0:2] - top)
            sums[0] += one[2:4] * factor
            sums[1] += one[4:6] * factor
            sums[2] += one[6:8]
        return top, sums

    quarters = pairs // 2
    ex_x[x] = stats[x]
    for i in (1, 2, 3):
        xo = lax.rem(x + i, NX)
        pltpu.make_async_remote_copy(
            src_ref=stats.at[xo], dst_ref=ex_x.at[x], send_sem=ssend.at[3], recv_sem=sex.at[0],
            device_id=tensor_at(z, xo), device_id_type=MESH,
        ).start()
    got(ex_x.at[pl.ds(0, NX - 1)], sex.at[0])
    top, sums = combine([ex_x[i] for i in range(NX)])
    ex_z[z] = jnp.concatenate([top + jnp.log(sums[0]), sums[1] / sums[0], sums[2]], axis=0)
    for i in range(1, nz):
        push(ex_z.at[z], ssend.at[4], sex.at[1], tensor_at(lax.rem(z + i, nz), x))
    got(ex_z.at[pl.ds(0, nz - 1)], sex.at[1])
    held = [ex_z[i] for i in range(nz)]
    top = functools.reduce(jnp.maximum, [one[0:2] for one in held])
    shares = [jnp.exp(one[0:2] - top) for one in held]
    total = sum(shares)
    lse = top + jnp.log(total)
    done[x, 0:2, :] = sum(one[4:6] for one in held) - lse
    done[x, 2:4, :] = lse - sum(share * one[2:4] for share, one in zip(shares, held)) / total
    for i in (1, 2, 3):
        push(done.at[x], ssend.at[5], sex.at[2], tensor_at(z, lax.rem(x + i, NX)))
    got(done.at[pl.ds(0, NX - 1)], sex.at[2])
    group_logp = jnp.concatenate([done[i, 0:2] for i in range(quarters)], axis=0)
    shape = group_logp.shape
    per = LANES // own_rows
    turn = lax.rem(LANES - t % per * own_rows, LANES)
    for s in range(2):
        line = done[t // per // 2, pl.ds(2 * s + t // per % 2, 1), :]
        out_ref[s:s + 1, :] = pltpu.roll(jnp.broadcast_to(line, (8, LANES)), turn, 1)[0:1, :]

    position = lax.broadcasted_iota(jnp.int32, shape, 0) * LANES + lax.broadcasted_iota(jnp.int32, shape, 1)
    count = lens_ref.shape[1]
    slot = lax.broadcasted_iota(jnp.int32, (1, LANES), 1)
    sums = jnp.zeros((1, LANES), jnp.float32)
    spans = jnp.ones((1, LANES), jnp.int32)
    start = jnp.int32(0)
    for q in range(count):
        end = start + lens_ref[0, q]
        inside = (position >= start) & (position < end)
        part = jnp.sum(jnp.sum(jnp.where(inside, group_logp, 0.0), axis=0, keepdims=True), axis=1, keepdims=True)
        sums = jnp.where(slot == q, part, sums)
        spans = jnp.where(slot == q, lens_ref[0, q], spans)
        start = end
    out_ref[2:3, :] = sums / spans.astype(jnp.float32)
    out_ref[3:8, :] = jnp.zeros((5, LANES), jnp.float32)

    for i in range(2):
        got(rows.at[pl.ds(0, nz - 1), 0, :, b_cols[i]], ssend.at[i])
    got(rows.at[pl.ds(0, nz - 1), :, :, pl.ds(0, ca)], ssend.at[9])
    got(rows.at[0, pl.ds(0, 3), :, pl.ds(0, ca)], ssend.at[2])
    got(rows.at[:, pl.ds(0, 2), :, pl.ds(ca, wide - ca)], ssend.at[8])
    got(rows.at[:, 0, :, b_cols[0]], ssend.at[10])
    got(rows.at[:, 0, :, b_cols[1]], ssend.at[11])
    got(wts.at[pl.ds(0, 3)], ssend.at[6])
    got(wts.at[pl.ds(0, 4)], ssend.at[7])
    got(ex_x.at[pl.ds(0, NX - 1)], ssend.at[3])
    got(ex_z.at[pl.ds(0, nz - 1)], ssend.at[4])
    got(done.at[pl.ds(0, NX - 1)], ssend.at[5])


def on_device(nz, hidden_states, norm_gain, head_weight, targets, lengths):
    own_rows, width = hidden_states.shape
    depth, vocab = head_weight.shape
    wide = width + LANES
    group_rows = nz * NX * own_rows
    vmem = pl.BlockSpec(memory_space=pltpu.VMEM)
    hbm = pl.BlockSpec(memory_space=pltpu.HBM)
    dma = pltpu.SemaphoreType.DMA
    out = pl.pallas_call(
        functools.partial(kernel, nz),
        out_shape=jax.ShapeDtypeStruct((8, LANES), jnp.float32),
        in_specs=[hbm] * 5,
        out_specs=vmem,
        scratch_shapes=[
            pltpu.VMEM((own_rows, width), jnp.bfloat16),
            pltpu.VMEM((width // LANES, LANES), jnp.float32),
            pltpu.SMEM((own_rows,), jnp.int32),
            pltpu.SMEM(lengths.shape, jnp.int32),
            pltpu.VMEM((nz, NX, own_rows, wide), jnp.bfloat16),
            pltpu.VMEM((2 * NY, CHUNKS, depth // CHUNKS, vocab), jnp.bfloat16),
            pltpu.VMEM((256, vocab), jnp.float32),
            pltpu.VMEM((group_rows // LANES // 2, 8, LANES), jnp.float32),
            pltpu.VMEM((NX, 8, LANES), jnp.float32),
            pltpu.VMEM((nz, 6, LANES), jnp.float32),
            pltpu.VMEM((NX, 4, LANES), jnp.float32),
            dma((2, 2, nz // 2 + 1)),
            dma((2, 4, nz // 2 + 1)),
            dma((3,)),
            dma((2, nz)),
            dma((2, nz)),
            dma((2, EVENTS)),
            dma((3, EVENTS)),
            dma((3,)),
            dma((12,)),
            dma((5,)),
        ],
        compiler_params=pltpu.CompilerParams(
            collective_id=0, has_side_effects=True, vmem_limit_bytes=64 << 20
        ),
    )(hidden_states, norm_gain.reshape(width // LANES, LANES),
      head_weight.reshape(CHUNKS, depth // CHUNKS, vocab), targets, lengths)
    return out[0, :own_rows], out[1, :own_rows], out[2:3, :lengths.shape[1]]


def solution(mesh):
    in_specs = (
        P(("dp", "tensor"), None),
        P(),
        P("dp", "tensor"),
        P(("dp", "tensor")),
        P("dp", None),
    )
    out_specs = (P(("dp", "tensor")), P(("dp", "tensor")), P("dp", None))
    return jax.shard_map(
        functools.partial(on_device, mesh.shape["tensor"] // NX),
        mesh=mesh, in_specs=in_specs, out_specs=out_specs, check_vma=False,
    )
```

```python
import functools

import jax
import jax.numpy as jnp
from jax import lax
from jax.experimental import pallas as pl
from jax.experimental.pallas import tpu as pltpu
from jax.sharding import PartitionSpec as P

MESH = pl.DeviceIdType.MESH
NX = 4
NY = 4
LANES = 128
CHUNKS = 4
EVENTS = 6


def split_columns(width):
    tiles = width // LANES
    first = max(1, round(tiles * 0.4)) * LANES
    rest = (width - first) // LANES
    return first, first + rest // 2 * LANES


def kernel(nz, hidden_hbm, gain_hbm, w_hbm, targets_hbm, lens_hbm,
           out_ref,
           hidden_ref, gain_ref, targets_ref, lens_ref,
           rows, ids, wts, logits, stats, ex_x, ex_z, done, si_x, si_z, sz_b, sz_a, sx_a, sx1, sx2, sw, sc, sex, ssend, sload):
    own_rows, width = hidden_ref.shape
    vocab = w_hbm.shape[-1]
    half = nz // 2
    ca, cm = split_columns(width)
    wide = width

    t = lax.axis_index("tensor")
    d = lax.axis_index("dp")
    z, x = t // NX, t % NX
    y, c = d // 2, d % 2

    def tensor_at(zz, xx):
        return {"tensor": zz * NX + xx}

    def dp_at(yy, cc):
        return {"dp": yy * 2 + cc}

    right, left = lax.rem(x + 1, NX), lax.rem(x + NX - 1, NX)
    across = lax.rem(x + 2, NX)
    up, down = lax.rem(z + 1, nz), lax.rem(z + nz - 1, nz)
    north, south = lax.rem(y + 1, NY), lax.rem(y + NY - 1, NY)

    loads = [
        pltpu.make_async_copy(src, dst, sload.at[i])
        for i, (src, dst) in enumerate((
            (hidden_hbm, hidden_ref), (gain_hbm, gain_ref), (targets_hbm, targets_ref),
            (lens_hbm, lens_ref), (w_hbm, wts.at[d])))
    ]
    for load in loads:
        load.start()

    barrier = pltpu.get_barrier_semaphore()
    peers = [tensor_at(z, right), tensor_at(z, left), tensor_at(z, across),
             tensor_at(up, x), tensor_at(down, x),
             dp_at(north, c), dp_at(south, c), dp_at(y, 1 - c)]
    for peer in peers:
        pl.semaphore_signal(barrier, inc=1, device_id=peer, device_id_type=MESH)

    for load in loads[:4]:
        load.wait()
    widths = hidden_ref[...].astype(jnp.float32)
    meansq = jnp.sum(widths * widths, axis=1, keepdims=True) / width
    scaled = widths * lax.rsqrt(meansq + 1e-06)
    for i in range(width // LANES):
        cols = slice(i * LANES, (i + 1) * LANES)
        rows[z, x, :, cols] = (scaled[:, cols] * gain_ref[i:i + 1, :]).astype(jnp.bfloat16)
    lane = lax.broadcasted_iota(jnp.int32, (1, LANES), 1)
    own_ids = jnp.zeros((1, LANES), jnp.int32)
    for i in range(own_rows):
        own_ids = jnp.where(lane == i, targets_ref[i], own_ids)
    ids[z, x] = own_ids.astype(jnp.float32)

    pl.semaphore_wait(barrier, len(peers))

    def push(ref, send, recv, peer):
        pltpu.make_async_remote_copy(
            src_ref=ref, dst_ref=ref, send_sem=send, recv_sem=recv,
            device_id=peer, device_id_type=MESH,
        ).start()

    def got(ref, sem):
        pltpu.make_async_copy(ref, ref, sem).wait()

    b_cols = (pl.ds(ca, cm - ca), pl.ds(cm, wide - cm))

    def b_piece(zo, i):
        return rows.at[zo, x, :, b_cols[i]]

    def a_piece(zo, i):
        return rows.at[zo, lax.rem(x + (0, 1, 3, 2)[i], NX), :, pl.ds(0, ca)]

    def send_b(zo, to, way, step, i):
        push(b_piece(zo, i), ssend.at[i], sz_b.at[way, i, step], tensor_at(to, x))

    def send_a(zo, to, way, step, i):
        push(a_piece(zo, i), ssend.at[9], sz_a.at[way, i, step], tensor_at(to, x))

    def send_x(zo):
        block = rows.at[zo, x, :, pl.ds(ca, wide - ca)]
        push(block, ssend.at[8], sx1.at[0, zo], tensor_at(z, right))
        push(block, ssend.at[8], sx1.at[1, zo], tensor_at(z, left))

    def send_across(zo):
        for i in range(2):
            push(b_piece(zo, i), ssend.at[10 + i], sx2.at[i, zo], tensor_at(z, across))

    def got_sides(zo):
        got(rows.at[zo, left, :, pl.ds(ca, wide - ca)], sx1.at[0, zo])
        got(rows.at[zo, right, :, pl.ds(ca, wide - ca)], sx1.at[1, zo])

    def forward_x(zo):
        got(rows.at[zo, left, :, pl.ds(ca, wide - ca)], sx1.at[0, zo])
        push(rows.at[zo, left, :, pl.ds(ca, cm - ca)], ssend.at[10], sx2.at[0, zo], tensor_at(z, right))
        got(rows.at[zo, right, :, pl.ds(ca, wide - ca)], sx1.at[1, zo])
        push(rows.at[zo, right, :, pl.ds(cm, wide - cm)], ssend.at[11], sx2.at[1, zo], tensor_at(z, left))

    def weight_event(j):
        for way in (0, 1):
            hop = 1 + j // CHUNKS
            yo = lax.rem(y + (NY - hop if way == 0 else hop), NY)
            piece = lax.rem(j + 2 * way, CHUNKS)
            ref = wts.at[yo * 2 + c, piece]
            got(ref, sw.at[way, j])

            @pl.when(j < 2)
            def _():
                push(ref, ssend.at[6], sw.at[way, j + CHUNKS], dp_at(north if way == 0 else south, c))

            push(ref, ssend.at[7], sc.at[way, j], dp_at(y, 1 - c))

    for i in range(2):
        send_b(z, up, 0, 1, i)
        send_b(z, down, 1, 1, i)
    loads[4].wait()
    for j in range(CHUNKS):
        push(wts.at[d, j], ssend.at[6], sw.at[0, j], dp_at(north, c))
        piece = (j + 2) % CHUNKS
        push(wts.at[d, piece], ssend.at[6], sw.at[1, j], dp_at(south, c))
    for i, (xo, slot) in enumerate(((right, 0), (left, 1), (across, 2))):
        push(rows.at[z, x, :, pl.ds(0, ca)], ssend.at[2], sx_a.at[slot], tensor_at(z, xo))
        push(ids.at[z, x], ssend.at[12], si_x.at[slot], tensor_at(z, xo))
    send_x(z)
    send_a(z, up, 0, 1, 0)
    send_a(z, down, 1, 1, 0)
    for j in range(CHUNKS):
        push(wts.at[d, j], ssend.at[7], sc.at[2, j], dp_at(y, 1 - c))
    for i, (xo, slot) in enumerate(((right, 1), (left, 0), (across, 2))):
        got(rows.at[z, xo, :, pl.ds(0, ca)], sx_a.at[slot])
        send_a(z, up, 0, 1, i + 1)
        send_a(z, down, 1, 1, i + 1)
    for xo, slot in ((right, 1), (left, 0), (across, 2)):
        got(ids.at[z, xo], si_x.at[slot])
    push(ids.at[z], ssend.at[13], si_z.at[0, 1], tensor_at(up, x))
    push(ids.at[z], ssend.at[13], si_z.at[1, 1], tensor_at(down, x))

    def ring_step(k, _):
        below, above = lax.rem(z + nz - k, nz), lax.rem(z + k, nz)
        for i in range(2):
            got(b_piece(below, i), sz_b.at[0, i, k])

            @pl.when((k < half - 1) | (i == 0))
            def _():
                send_b(below, up, 0, k + 1, i)

            got(b_piece(above, i), sz_b.at[1, i, k])

            @pl.when((k < half - 1) | (i == 1))
            def _():
                send_b(above, down, 1, k + 1, i)

        send_x(below)
        send_x(above)

        @pl.when(k == half - 1)
        def _():
            send_across(below)
            send_across(above)

        for i in range(4):
            got(a_piece(below, i), sz_a.at[0, i, k])

            @pl.when((k < half - 1) | (i < 2))
            def _():
                send_a(below, up, 0, k + 1, i)

            got(a_piece(above, i), sz_a.at[1, i, k])

            @pl.when((k < half - 1) | (i >= 2))
            def _():
                send_a(above, down, 1, k + 1, i)

        got(ids.at[below], si_z.at[0, k])
        push(ids.at[below], ssend.at[13], si_z.at[0, k + 1], tensor_at(up, x))
        got(ids.at[above], si_z.at[1, k])

        @pl.when(k < half - 1)
        def _():
            push(ids.at[above], ssend.at[13], si_z.at[1, k + 1], tensor_at(down, x))

        forward_x(lax.rem(z + nz - k + 1, nz))

        @pl.when(k > 1)
        def _():
            forward_x(lax.rem(z + k - 1, nz))

        @pl.when(k <= EVENTS)
        def _():
            weight_event(k - 1)

        return 0

    lax.fori_loop(1, half, ring_step, 0)
    far = lax.rem(z + half, nz)
    got(b_piece(far, 0), sz_b.at[0, 0, half])
    got(b_piece(far, 1), sz_b.at[1, 1, half])
    send_x(far)
    send_across(far)
    for j in range(half - 1, EVENTS):
        weight_event(jnp.int32(j))

    def last_w(j, _):
        got(wts.at[0, 0], sc.at[0, j])
        got(wts.at[0, 0], sc.at[1, j])
        return 0

    lax.fori_loop(0, EVENTS, last_w, 0)
    for j in range(CHUNKS):
        got(wts.at[0, 0], sc.at[2, j])

    pairs = nz // 2
    pair_rows = 2 * NX * own_rows
    vocab_start = t * vocab
    def pairs_of(j):
        return lax.rem(z // 2 + pairs - j, pairs), lax.rem(z // 2 + 1 + j, pairs)

    def arrived(j):
        if j == pairs // 2 - 2:
            got_sides(lax.rem(z + nz - half + 1, nz))
            got_sides(lax.rem(z + half - 1, nz))
        if j == pairs // 2 - 1:
            for i in range(4):
                got(a_piece(far, i), sz_a.at[i // 2, i, half])
            got_sides(far)
            got(ids.at[far], si_z.at[0, half])
        for pair in pairs_of(j):
            for i in range(2):
                zo = pair * 2 + i
                got(rows.at[zo, across, :, b_cols[0]], sx2.at[0, zo])
                got(rows.at[zo, across, :, b_cols[1]], sx2.at[1, zo])

    def multiply(j):
        held = [rows[pl.ds(pair * 2, 2)].reshape(pair_rows, wide) for pair in pairs_of(j)]
        held = jnp.concatenate(held, axis=0)
        rhs = wts[...].reshape(width, vocab)
        logits[...] = jnp.dot(held[:, 0:width], rhs, preferred_element_type=jnp.float32)

    def summarize(j):
        both = pairs_of(j)
        spread = jnp.concatenate(
            [jnp.broadcast_to(ids[pl.ds(pair * 2, 2)], (2, NX, own_rows, LANES)).reshape(pair_rows, LANES)
             for pair in both], axis=0)
        row = lax.rem(lax.broadcasted_iota(jnp.int32, spread.shape, 0), own_rows)
        own_lane = lax.broadcasted_iota(jnp.int32, spread.shape, 1) == row
        wanted = jnp.sum(jnp.where(own_lane, spread, 0.0), axis=1, keepdims=True).astype(jnp.int32) - vocab_start
        values = logits[...]
        highest = jnp.max(values, axis=1, keepdims=True)
        expo = jnp.exp(values - highest)
        total = jnp.sum(expo, axis=1, keepdims=True)
        weighted = jnp.sum(expo * values, axis=1, keepdims=True)
        columns = lax.broadcasted_iota(jnp.int32, values.shape, 1)
        picked = jnp.sum(jnp.where(columns == wanted, values, 0.0), axis=1, keepdims=True)
        at = lax.broadcasted_iota(jnp.int32, (2 * pair_rows, LANES), 1)
        table = jnp.where(at == 0, highest, jnp.where(at == 1, total, jnp.where(at == 2, weighted, picked)))
        flat = jnp.transpose(table)
        for i, pair in enumerate(both):
            for s in range(4):
                stats[pair // 2, pl.ds(2 * s + pair % 2, 1), :] = flat[s:s + 1, i * LANES:(i + 1) * LANES]

    def score(j, _):
        for jj in range(pairs // 2):
            @pl.when(j == jj)
            def _():
                arrived(jj)

        multiply(j)
        summarize(j)
        return 0

    lax.fori_loop(0, pairs // 2, score, 0)

    def combine(held):
        top = held[0][0:2]
        for one in held[1:]:
            top = jnp.maximum(top, one[0:2])
        sums = [jnp.zeros_like(top) for _ in range(3)]
        for one in held:
            factor = jnp.exp(one[0:2] - top)
            sums[0] += one[2:4] * factor
            sums[1] += one[4:6] * factor
            sums[2] += one[6:8]
        return top, sums

    quarters = pairs // 2
    ex_x[x] = stats[x]
    for i in (2, 1, 3):
        xo = lax.rem(x + i, NX)
        pltpu.make_async_remote_copy(
            src_ref=stats.at[xo], dst_ref=ex_x.at[x], send_sem=ssend.at[3], recv_sem=sex.at[0],
            device_id=tensor_at(z, xo), device_id_type=MESH,
        ).start()
    got(ex_x.at[pl.ds(0, NX - 1)], sex.at[0])
    top, sums = combine([ex_x[i] for i in range(NX)])
    ex_z[z] = jnp.concatenate([top + jnp.log(sums[0]), sums[1] / sums[0], sums[2]], axis=0)
    for i in sorted(range(1, nz), key=lambda i: -min(i, nz - i)):
        push(ex_z.at[z], ssend.at[4], sex.at[1], tensor_at(lax.rem(z + i, nz), x))
    got(ex_z.at[pl.ds(0, nz - 1)], sex.at[1])
    held = [ex_z[i] for i in range(nz)]
    top = functools.reduce(jnp.maximum, [one[0:2] for one in held])
    shares = [jnp.exp(one[0:2] - top) for one in held]
    total = sum(shares)
    lse = top + jnp.log(total)
    done[x, 0:2, :] = sum(one[4:6] for one in held) - lse
    done[x, 2:4, :] = lse - sum(share * one[2:4] for share, one in zip(shares, held)) / total
    for i in (2, 1, 3):
        push(done.at[x], ssend.at[5], sex.at[2], tensor_at(z, lax.rem(x + i, NX)))
    got(done.at[pl.ds(0, NX - 1)], sex.at[2])
    group_logp = jnp.concatenate([done[i, 0:2] for i in range(quarters)], axis=0)
    shape = group_logp.shape
    per = LANES // own_rows
    turn = lax.rem(LANES - t % per * own_rows, LANES)
    for s in range(2):
        line = done[t // per // 2, pl.ds(2 * s + t // per % 2, 1), :]
        out_ref[s:s + 1, :] = pltpu.roll(jnp.broadcast_to(line, (8, LANES)), turn, 1)[0:1, :]

    position = lax.broadcasted_iota(jnp.int32, shape, 0) * LANES + lax.broadcasted_iota(jnp.int32, shape, 1)
    count = lens_ref.shape[1]
    slot = lax.broadcasted_iota(jnp.int32, (1, LANES), 1)
    sums = jnp.zeros((1, LANES), jnp.float32)
    spans = jnp.ones((1, LANES), jnp.int32)
    start = jnp.int32(0)
    for q in range(count):
        end = start + lens_ref[0, q]
        inside = (position >= start) & (position < end)
        part = jnp.sum(jnp.sum(jnp.where(inside, group_logp, 0.0), axis=0, keepdims=True), axis=1, keepdims=True)
        sums = jnp.where(slot == q, part, sums)
        spans = jnp.where(slot == q, lens_ref[0, q], spans)
        start = end
    out_ref[2:3, :] = sums / spans.astype(jnp.float32)
    out_ref[3:8, :] = jnp.zeros((5, LANES), jnp.float32)

    for i in range(2):
        got(rows.at[pl.ds(0, nz - 1), 0, :, b_cols[i]], ssend.at[i])
    got(rows.at[pl.ds(0, nz - 1), :, :, pl.ds(0, ca)], ssend.at[9])
    got(rows.at[0, pl.ds(0, 3), :, pl.ds(0, ca)], ssend.at[2])
    got(rows.at[:, pl.ds(0, 2), :, pl.ds(ca, wide - ca)], ssend.at[8])
    got(rows.at[:, 0, :, b_cols[0]], ssend.at[10])
    got(rows.at[:, 0, :, b_cols[1]], ssend.at[11])
    got(wts.at[pl.ds(0, 3)], ssend.at[6])
    got(wts.at[pl.ds(0, 4)], ssend.at[7])
    got(ids.at[0, pl.ds(0, 3)], ssend.at[12])
    got(ids.at[pl.ds(0, nz - 1)], ssend.at[13])
    got(ex_x.at[pl.ds(0, NX - 1)], ssend.at[3])
    got(ex_z.at[pl.ds(0, nz - 1)], ssend.at[4])
    got(done.at[pl.ds(0, NX - 1)], ssend.at[5])


def on_device(nz, hidden_states, norm_gain, head_weight, targets, lengths):
    own_rows, width = hidden_states.shape
    depth, vocab = head_weight.shape
    group_rows = nz * NX * own_rows
    vmem = pl.BlockSpec(memory_space=pltpu.VMEM)
    hbm = pl.BlockSpec(memory_space=pltpu.HBM)
    dma = pltpu.SemaphoreType.DMA
    out = pl.pallas_call(
        functools.partial(kernel, nz),
        out_shape=jax.ShapeDtypeStruct((8, LANES), jnp.float32),
        in_specs=[hbm] * 5,
        out_specs=vmem,
        scratch_shapes=[
            pltpu.VMEM((own_rows, width), jnp.bfloat16),
            pltpu.VMEM((width // LANES, LANES), jnp.float32),
            pltpu.SMEM((own_rows,), jnp.int32),
            pltpu.SMEM(lengths.shape, jnp.int32),
            pltpu.VMEM((nz, NX, own_rows, width), jnp.bfloat16),
            pltpu.VMEM((nz, NX, 1, LANES), jnp.float32),
            pltpu.VMEM((2 * NY, CHUNKS, depth // CHUNKS, vocab), jnp.bfloat16),
            pltpu.VMEM((256, vocab), jnp.float32),
            pltpu.VMEM((group_rows // LANES // 2, 8, LANES), jnp.float32),
            pltpu.VMEM((NX, 8, LANES), jnp.float32),
            pltpu.VMEM((nz, 6, LANES), jnp.float32),
            pltpu.VMEM((NX, 4, LANES), jnp.float32),
            dma((3,)),
            dma((2, nz // 2 + 1)),
            dma((2, 2, nz // 2 + 1)),
            dma((2, 4, nz // 2 + 1)),
            dma((3,)),
            dma((2, nz)),
            dma((2, nz)),
            dma((2, EVENTS)),
            dma((3, EVENTS)),
            dma((3,)),
            dma((14,)),
            dma((5,)),
        ],
        compiler_params=pltpu.CompilerParams(
            collective_id=0, has_side_effects=True, vmem_limit_bytes=64 << 20
        ),
    )(hidden_states, norm_gain.reshape(width // LANES, LANES),
      head_weight.reshape(CHUNKS, depth // CHUNKS, vocab), targets, lengths)
    return out[0, :own_rows], out[1, :own_rows], out[2:3, :lengths.shape[1]]


def solution(mesh):
    in_specs = (
        P(("dp", "tensor"), None),
        P(),
        P("dp", "tensor"),
        P(("dp", "tensor")),
        P("dp", None),
    )
    out_specs = (P(("dp", "tensor")), P(("dp", "tensor")), P("dp", None))
    return jax.shard_map(
        functools.partial(on_device, mesh.shape["tensor"] // NX),
        mesh=mesh, in_specs=in_specs, out_specs=out_specs, check_vma=False,
    )
```
